32 devices in a mesh: grp: 4 (over x, core), vec: 8 (over z, y).
Axes of the slice: x: 2, y: 2, z: 4, core: 2. Of those that a mesh axis runs over, the one named last changes fastest.
Arguments:
- vv_vectors: bfloat16 [1280, 1000, 1000], P(('grp', 'vec')), may hold values from -0.1875 to 0.1875
- oo_vectors: bfloat16 [1280, 100, 100], P(('grp', 'vec')), may hold values from -0.625 to 0.625
- ov_slab: bfloat16 [1280, 1024], P(('grp', 'vec')), may hold values from -0.15625 to 0.15625
- amplitudes: bfloat16 [100, 1000], P('grp'), may hold values from -6 to 6
Outputs:
- sigma_slab: float32 [96000, 1024], P(('grp', 'vec'))
The draws below stay inside these ranges and needn't reach their ends.
All inputs are finite; a program needn't handle non-finite values.
Results may differ from the reference program's by a relative error of at most 0.0029.
Values may be sent and summed in bfloat16 or wider, within the bound.
A program may use at most 192 MiB of HBM per device.

```python
import math
import jax
import jax.numpy as jnp
from jax import lax

NO = 100
NV = 1000
NP = 1280
I_ROWS = 96
SLAB = 1024


def level_of(key, dims, split, low, largest):
    level = 1.0
    for axis_at, parts in split:
        heights = jax.random.uniform(jax.random.fold_in(jax.random.fold_in(key, 6), axis_at), (parts,), jnp.float32, low / len(split), largest / len(split))
        level = level * jnp.repeat(jnp.exp(heights), dims[axis_at] // parts).reshape((-1,) + (1,) * (len(dims) - 1 - axis_at))
    return level


def gaussian(own_key, extent, scale, reach, shards=(), held_as=jnp.bfloat16):
    entries = jax.random.normal(own_key, extent, jnp.float32) * scale
    if len(shards) > 0:
        entries = level_of(own_key, extent, shards, -0.22, 0.18) * entries
    return jnp.clip(entries, min=-reach, max=reach).astype(held_as)


def setup_inputs(seed: int = 0) -> dict:
    keys = jax.random.split(jax.random.key(seed), 5)
    vv_vectors = gaussian(keys[0], (NP, NV, NV), NV ** -0.5, 0.1875, ((0, 32),))
    oo_vectors = gaussian(keys[1], (NP, NO, NO), NO ** -0.5, 0.625, ((0, 32),))
    ov_slab = gaussian(keys[2], (NP, SLAB), NP ** -0.5, 0.15625, ((0, 32),))
    amplitudes = gaussian(keys[3], (NO, NV), 1.0, 6.0, ((0, 4),))
    return {"vv_vectors": vv_vectors, "oo_vectors": oo_vectors, "ov_slab": ov_slab, "amplitudes": amplitudes}


def reference(vv_vectors, oo_vectors, ov_slab, amplitudes):
    block_size = math.gcd(NP, 64)
    window = amplitudes[:I_ROWS].astype(jnp.float32)
    amps_all = amplitudes.astype(jnp.float32)

    def accumulate(running, counter):
        offset = (counter * block_size).astype(jnp.int32)
        vv_block = lax.dynamic_slice_in_dim(vv_vectors, offset, block_size, 0).astype(jnp.float32)
        oo_block = lax.dynamic_slice_in_dim(oo_vectors, offset, block_size, 0)[:, :, :I_ROWS].astype(jnp.float32)
        ov_part = lax.dynamic_slice_in_dim(ov_slab, offset, block_size, 0)
        direct_term = jnp.einsum('ib,pab->pia', window, vv_block)
        hole_term = jnp.einsum('pji,ja->pia', oo_block, amps_all)
        dressed = (direct_term - hole_term).astype(jnp.bfloat16).reshape(block_size, I_ROWS * NV)
        update = lax.dot_general(dressed, ov_part, (((0,), (0,)), ((), ())), preferred_element_type=jnp.float32)
        return running + update, None

    start_sum = jnp.zeros((I_ROWS * NV, SLAB), jnp.float32)
    running, _ = lax.scan(accumulate, start_sum, jnp.arange(NP // block_size, dtype=jnp.int32))
    return running
```

```python
import functools
import jax
import jax.numpy as jnp
from jax import lax
from jax.experimental import pallas as pl
from jax.experimental.pallas import tpu as pltpu
from jax.sharding import PartitionSpec as P

I_ROWS = 96
CHUNK = 8
BLOCK = 256
LANES = 128
COLUMNS = 256
LIMIT_MIB = 28
FINISH_MIB = 8
MESH = pl.DeviceIdType.MESH


def farthest_first(count):
    return sorted(range(count), key=lambda k: (abs(k - count // 2), k))


def exchange_kernel(
    ng, nv, inner, amps, oo, ov, vv, partial, received, slab,
    vv_slots, oo_here, oo_f32, oo_turned, stage, dressed, gathered, rows_f32, amps_all,
    vv_sem, send_sem, recv_sem, own_sem, oo_sem, far_sems, near_sems, plane_send, plane_recv, slab_sem,
    amps_send, amps_recv, amps_own,
):
    g = lax.axis_index("grp")
    v = lax.axis_index("vec")
    me = g * nv + v
    local_count, nvirt = vv.shape[0], vv.shape[1]
    nocc = oo.shape[0]
    chunks = local_count // CHUNK
    blocks = -(-nvirt // BLOCK)
    widths = [min(BLOCK, nvirt - b * BLOCK) for b in range(blocks)]
    per = I_ROWS // (ng * nv)
    depth = ng * nv * CHUNK
    outer = nv // inner
    half = outer // 2
    z = v // inner
    y = lax.rem(v, inner)
    z_far = lax.rem(z + half, outer)
    held = amps.shape[0]
    order = [(dv, dg) for dv in farthest_first(nv) for dg in range(ng) if (dg, dv) != (0, 0)]
    plane = [(dg, dy) for dg in range(ng) for dy in range(inner) if (dg, dy) != (0, 0)]

    def load(c, b):
        return pltpu.make_async_copy(
            vv.at[pl.ds(pl.multiple_of(c * CHUNK, CHUNK), CHUNK), pl.ds(b * BLOCK, widths[b])],
            vv_slots.at[b, :, pl.ds(0, widths[b])],
            vv_sem.at[b],
        )

    barrier = pltpu.get_barrier_semaphore()
    for dv, dg in order:
        pl.semaphore_signal(
            barrier, inc=1, device_id=(lax.rem(g + dg, ng), lax.rem(v + dv, nv)), device_id_type=MESH
        )
    own_amps = pltpu.make_async_copy(amps, gathered.at[g], amps_own)
    own_amps.start()
    own_oo = pltpu.make_async_copy(oo, oo_here, oo_sem)
    own_oo.start()

    def piece(at_z):
        return slab.at[:, g, at_z, pl.ds(pl.multiple_of(y * CHUNK, CHUNK), CHUNK)]

    own_slab = pltpu.make_async_copy(ov, piece(z), slab_sem)
    own_slab.start()
    for b in range(blocks):
        load(0, b).start()

    def turn(c):
        eight = oo_here[:, pl.ds(pl.multiple_of(c * CHUNK, CHUNK), CHUNK), :].astype(jnp.float32)
        oo_f32[:, 0:eight.shape[2]] = eight.reshape(nocc * CHUNK, eight.shape[2])
        for k in range(CHUNK):
            one = oo_f32[pl.ds(k, nocc, stride=CHUNK), :]
            oo_turned[k, :, 0:nocc] = one.T[0:I_ROWS, :].astype(jnp.bfloat16)

    own_oo.wait()
    oo_f32[...] = jnp.zeros_like(oo_f32)
    stage[...] = jnp.zeros_like(stage)
    turn(0)
    pl.semaphore_wait(barrier, len(order))

    def amps_copy(dg):
        return pltpu.make_async_remote_copy(
            src_ref=amps,
            dst_ref=gathered.at[g],
            send_sem=amps_send.at[dg],
            recv_sem=amps_recv.at[dg],
            device_id=(lax.rem(g + dg, ng), v),
            device_id_type=MESH,
        )

    far_copy = pltpu.make_async_remote_copy(
        src_ref=ov,
        dst_ref=piece(z),
        send_sem=far_sems.at[0],
        recv_sem=far_sems.at[1],
        device_id=(g, z_far * inner + y),
        device_id_type=MESH,
    )

    def near_copy(dz, which):
        at_z = (z, z_far)[which]
        return pltpu.make_async_remote_copy(
            src_ref=piece(at_z),
            dst_ref=piece(at_z),
            send_sem=near_sems.at[0, which, dz],
            recv_sem=near_sems.at[1, which, dz],
            device_id=(g, ((z // half) * half + lax.rem(z + dz, half)) * inner + y),
            device_id_type=MESH,
        )

    def plane_copy(j):
        dg, dy = plane[j]
        column = slab.at[:, g, :, pl.ds(pl.multiple_of(y * CHUNK, CHUNK), CHUNK)]
        return pltpu.make_async_remote_copy(
            src_ref=column,
            dst_ref=column,
            send_sem=plane_send.at[j],
            recv_sem=plane_recv.at[j],
            device_id=(lax.rem(g + dg, ng), z * inner + lax.rem(y + dy, inner)),
            device_id_type=MESH,
        )

    for dg in range(1, ng):
        amps_copy(dg).start()
    far_copy.start()
    own_amps.wait()
    for dg in range(1, ng):
        amps_copy(dg).wait_send()
        amps_copy(dg).wait_recv()
    for s in range(ng):
        rows_f32[s * held:(s + 1) * held, :] = gathered[s].astype(jnp.float32)
    amps_all[...] = rows_f32[0:ng * held, :].astype(jnp.bfloat16)

    def owner(dv, dg):
        return lax.rem(g + dg, ng), lax.rem(v + nv + dv * (1 - 2 * lax.rem(g, 2)), nv)

    def dress(c, b):
        width = widths[b]
        lo = b * BLOCK
        load(c, b).wait()

        @pl.loop(0, CHUNK)
        def _(k):
            direct = lax.dot_general(
                amps_all[0:I_ROWS, :], vv_slots[b, k, 0:width, :], (((1,), (1,)), ((), ())),
                preferred_element_type=jnp.float32,
            )
            hole = lax.dot_general(
                oo_turned[k, :, 0:nocc], amps_all[:, lo:lo + width], (((1,), (0,)), ((), ())),
                preferred_element_type=jnp.float32,
            )
            value = direct - hole
            for t in range(-(-width // LANES)):
                at, to = t * LANES, min(t * LANES + LANES, width)
                stage[t, pl.ds(pl.multiple_of(k * I_ROWS, I_ROWS), I_ROWS), 0:to - at] = value[:, at:to]

        @pl.when(c + 1 < chunks)
        def _():
            load(c + 1, b).start()

        landing = received.at[c, b, :, pl.ds(pl.multiple_of(me * CHUNK, CHUNK), CHUNK)]

        def regroup(first):
            for i in range(per):
                for t in range(-(-width // LANES)):
                    rows = stage[t, pl.ds(first + i, CHUNK, stride=I_ROWS), :]
                    dressed[c, b, first + i, :, t * LANES:t * LANES + LANES] = rows.astype(jnp.bfloat16)

        def send(step):
            to_g, to_v = owner(*step)
            pltpu.make_async_remote_copy(
                src_ref=dressed.at[c, b, pl.ds((to_g * nv + to_v) * per, per)],
                dst_ref=landing,
                send_sem=send_sem,
                recv_sem=recv_sem.at[c, b],
                device_id=(to_g, to_v),
                device_id_type=MESH,
            ).start()

        for at, step in enumerate(order):
            to_g, to_v = owner(*step)
            regroup((to_g * nv + to_v) * per)
            if at >= 2:
                send(order[at - 2])
        regroup(me * per)
        send(order[-2])
        send(order[-1])
        pltpu.make_async_copy(dressed.at[c, b, pl.ds(me * per, per)], landing, own_sem.at[c, b]).start()

    @pl.loop(0, chunks)
    def _(c):
        for b in range(blocks):
            dress(c, b)
            if b == 0:
                @pl.when(c == 0)
                def _():
                    own_slab.wait()
                    far_copy.wait_send()
                    far_copy.wait_recv()
                    for dz in range(1, half):
                        near_copy(dz, 0).start()
                        near_copy(dz, 1).start()
            if b == 1:
                @pl.when(c == 0)
                def _():
                    for dz in range(1, half):
                        for which in range(2):
                            near_copy(dz, which).wait_send()
                            near_copy(dz, which).wait_recv()
                    for j in range(len(plane)):
                        plane_copy(j).start()

        @pl.when(c + 1 < chunks)
        def _():
            turn(c + 1)

    partial[...] = jnp.zeros_like(partial)
    for j in range(len(plane)):
        plane_copy(j).wait_send()
        plane_copy(j).wait_recv()

    def arrived(c, b):
        others = received.at[c, b, :, pl.ds(0, depth - CHUNK)]
        pltpu.make_async_copy(others, others, recv_sem.at[c, b]).wait()
        mine = received.at[c, b, :, pl.ds(0, CHUNK)]
        pltpu.make_async_copy(mine, mine, own_sem.at[c, b]).wait()

    def contract_block(c, b):
        rhs = slab[c].reshape(depth, slab.shape[-1])
        rows = pl.ds(b * BLOCK, widths[b])

        @pl.loop(0, per)
        def _(i):
            lhs = received[c, b, i, :, 0:widths[b]]
            for lo in range(0, slab.shape[-1], COLUMNS):
                partial[i, rows, lo:lo + COLUMNS] += lax.dot_general(
                    lhs, rhs[:, lo:lo + COLUMNS], (((0,), (0,)), ((), ())),
                    preferred_element_type=jnp.float32,
                )

    @pl.loop(0, chunks)
    def _(c):
        for b in range(blocks):
            arrived(c, b)
            if b < blocks - 1:
                contract_block(c, b)
            else:
                @pl.when(c + 1 < chunks)
                def _():
                    contract_block(c, b)

    sent = received.at[:, :, :, pl.ds(0, depth - CHUNK)]
    pltpu.make_async_copy(sent, sent, send_sem).wait()


def finish_kernel(partial, received, slab, out, tail, sems):
    last, block = received.shape[0] - 1, received.shape[1] - 1
    per, nvirt = partial.shape[0], partial.shape[1]
    lo = block * BLOCK
    copies = []

    def copy(src, dst):
        copies.append(pltpu.make_async_copy(src, dst, sems.at[len(copies)]))
        copies[-1].start()

    for i in range(per):
        copy(partial.at[i, 0:lo], out.at[i, 0:lo])
    rhs = slab[last].reshape(received.shape[3], slab.shape[-1])
    for i in range(per):
        tail[i] = partial[i, lo:, :] + lax.dot_general(
            received[last, block, i, :, 0:nvirt - lo], rhs, (((0,), (0,)), ((), ())),
            preferred_element_type=jnp.float32,
        )
        copy(tail.at[i], out.at[i, lo:])
    for one in copies:
        one.wait()


def contract(ng, nv, vv_vectors, oo_vectors, ov_slab, amplitudes):
    local_count, nvirt = vv_vectors.shape[0], vv_vectors.shape[1]
    width = ov_slab.shape[1]
    devices = ng * nv
    inner = 2
    outer = nv // inner
    chunks = local_count // CHUNK
    blocks = -(-nvirt // BLOCK)
    per = I_ROWS // devices
    nocc = ng * amplitudes.shape[0]
    hbm = pl.BlockSpec(memory_space=pltpu.HBM)
    vmem = pl.BlockSpec(memory_space=pltpu.VMEM)
    dma = pltpu.SemaphoreType.DMA
    stay = functools.partial(pltpu.with_memory_space_constraint, memory_space=pltpu.HBM)
    partial, received, slab = pl.pallas_call(
        functools.partial(exchange_kernel, ng, nv, inner),
        out_shape=(
            jax.ShapeDtypeStruct((per, nvirt, width), jnp.float32),
            jax.ShapeDtypeStruct((chunks, blocks, per, devices * CHUNK, BLOCK), jnp.bfloat16),
            jax.ShapeDtypeStruct((chunks, ng, outer, inner * CHUNK, width), jnp.bfloat16),
        ),
        in_specs=[hbm, hbm, hbm, hbm],
        out_specs=(vmem, vmem, vmem),
        scratch_shapes=[
            pltpu.VMEM((blocks, CHUNK, BLOCK, nvirt), jnp.bfloat16),
            pltpu.VMEM((nocc, local_count, nocc), jnp.bfloat16),
            pltpu.VMEM((nocc * CHUNK, LANES), jnp.float32),
            pltpu.VMEM((CHUNK, I_ROWS, LANES), jnp.bfloat16),
            pltpu.VMEM((BLOCK // LANES, CHUNK * I_ROWS, LANES), jnp.float32),
            pltpu.VMEM((chunks, blocks, I_ROWS, CHUNK, BLOCK), jnp.bfloat16),
            pltpu.VMEM((ng,) + amplitudes.shape, jnp.bfloat16),
            pltpu.VMEM((nocc, nvirt), jnp.float32),
            pltpu.VMEM((nocc, nvirt), jnp.bfloat16),
            dma((blocks,)),
            dma,
            dma((chunks, blocks)),
            dma((chunks, blocks)),
            dma,
            dma((2,)),
            dma((2, 2, outer // 2)),
            dma((ng * inner - 1,)),
            dma((ng * inner - 1,)),
            dma,
            dma((ng,)),
            dma((ng,)),
            dma,
        ],
        compiler_params=pltpu.CompilerParams(
            collective_id=0, has_side_effects=True, vmem_limit_bytes=LIMIT_MIB * 1024 * 1024
        ),
    )(
        stay(amplitudes), stay(jnp.transpose(oo_vectors, (1, 0, 2))),
        stay(ov_slab.reshape(chunks, CHUNK, width)), stay(vv_vectors),
    )
    return pl.pallas_call(
        finish_kernel,
        out_shape=jax.ShapeDtypeStruct((per, nvirt, width), jnp.float32),
        in_specs=[vmem, vmem, vmem],
        out_specs=hbm,
        scratch_shapes=[
            pltpu.VMEM((per, nvirt - (blocks - 1) * BLOCK, width), jnp.float32),
            dma((2 * per,)),
        ],
        compiler_params=pltpu.CompilerParams(vmem_limit_bytes=FINISH_MIB * 1024 * 1024),
    )(partial, received, slab).reshape(per * nvirt, width)


def plain(vv_vectors, oo_vectors, ov_slab, amps_all):
    local_count, nvirt = vv_vectors.shape[0], vv_vectors.shape[1]
    window = amps_all[:I_ROWS]
    direct_term = jnp.einsum("ib,pab->pia", window, vv_vectors, preferred_element_type=jnp.float32)
    hole_term = jnp.einsum(
        "pji,ja->pia", oo_vectors[:, :, :I_ROWS], amps_all, preferred_element_type=jnp.float32
    )
    dressed = (direct_term - hole_term).astype(jnp.bfloat16).reshape(local_count, I_ROWS * nvirt)
    regrouped = lax.all_to_all(dressed, ("grp", "vec"), split_axis=1, concat_axis=0, tiled=True)
    return lax.dot_general(
        regrouped,
        lax.all_gather(ov_slab, ("grp", "vec"), axis=0, tiled=True),
        (((0,), (0,)), ((), ())),
        preferred_element_type=jnp.float32,
    )


def solution(mesh):
    ng, nv = mesh.shape["grp"], mesh.shape["vec"]

    def shards(vv_vectors, oo_vectors, ov_slab, amplitudes):
        local_count, nvirt = vv_vectors.shape[0], vv_vectors.shape[1]
        fits = (
            I_ROWS % (ng * nv) == 0 and nv % 4 == 0 and local_count % CHUNK == 0 and nvirt % CHUNK == 0
            and oo_vectors.shape[1] <= LANES and ov_slab.shape[1] % COLUMNS == 0
        )
        if not fits:
            amps_all = lax.all_gather(amplitudes, "grp", axis=0, tiled=True)
            return plain(vv_vectors, oo_vectors, ov_slab, amps_all)
        return contract(ng, nv, vv_vectors, oo_vectors, ov_slab, amplitudes)

    return jax.shard_map(
        shards,
        mesh=mesh,
        in_specs=(
            P(("grp", "vec"), None, None),
            P(("grp", "vec"), None, None),
            P(("grp", "vec"), None),
            P("grp", None),
        ),
        out_specs=P(("grp", "vec"), None),
        check_vma=False,
    )
```

```python
import functools
import jax
import jax.numpy as jnp
from jax import lax
from jax.experimental import pallas as pl
from jax.experimental.pallas import tpu as pltpu
from jax.sharding import PartitionSpec as P

I_ROWS = 96
CHUNK = 8
BLOCK = 256
LANES = 128
ROWS = 8
COLUMNS = 256
LIMIT_MIB = 30
FINISH_MIB = 8
MESH = pl.DeviceIdType.MESH


def farthest_first(count):
    return sorted(range(count), key=lambda k: (abs(k - count // 2), k))


def packing(total, nvirt):
    rest = nvirt % LANES
    cells, room = rest // ROWS, (LANES - rest) // ROWS
    kept = -(-total * cells // (cells + room))
    return rest, cells, room, kept


def exchange_kernel(
    ng, nv, inner, amps, oo, ov, vv, partial, received, slab,
    packed, unpacked, vv_slots, oo_here, oo_f32, oo_turned, stage, dressed, gathered, rows_f32, amps_all,
    vv_sem, send_sem, recv_sem, own_sem, oo_sem, far_sems, near_sems, plane_send, plane_recv, slab_sem,
    amps_send, amps_recv, amps_own, rest_send, rest_recv, rest_own,
):
    g = lax.axis_index("grp")
    v = lax.axis_index("vec")
    me = g * nv + v
    local_count, nvirt = vv.shape[0], vv.shape[1]
    nocc = oo.shape[0]
    chunks = local_count // CHUNK
    blocks = -(-nvirt // BLOCK)
    widths = [min(BLOCK, nvirt - b * BLOCK) for b in range(blocks)]
    per = I_ROWS // (ng * nv)
    edge = blocks - 1
    slots = vv_slots.shape[0]
    rest, cells, room, kept = packing(chunks * per, nvirt)
    moved = chunks * per - kept
    full = [w // LANES * LANES for w in widths]
    depth = ng * nv * CHUNK
    outer = nv // inner
    half = outer // 2
    z = v // inner
    y = lax.rem(v, inner)
    z_far = lax.rem(z + half, outer)
    held = amps.shape[0]
    order = [(dv, dg) for dv in farthest_first(nv) for dg in range(ng) if (dg, dv) != (0, 0)]
    plane = [(dg, dy) for dg in range(ng) for dy in range(inner) if (dg, dy) != (0, 0)]

    def slot_of(c, b):
        if b == edge:
            return lax.rem(c + 1, slots)
        if b == 0:
            return lax.rem(jnp.where(c == 0, 0, chunks + edge * c), slots)
        return lax.rem(chunks + edge * c + b, slots)

    def load(c, b):
        return pltpu.make_async_copy(
            vv.at[pl.ds(pl.multiple_of(c * CHUNK, CHUNK), CHUNK), pl.ds(b * BLOCK, widths[b])],
            vv_slots.at[slot_of(c, b), :, pl.ds(0, widths[b])],
            vv_sem.at[slot_of(c, b)],
        )

    barrier = pltpu.get_barrier_semaphore()
    for dv, dg in order:
        pl.semaphore_signal(
            barrier, inc=1, device_id=(lax.rem(g + dg, ng), lax.rem(v + dv, nv)), device_id_type=MESH
        )
    own_amps = pltpu.make_async_copy(amps, gathered.at[g], amps_own)
    own_amps.start()
    own_oo = pltpu.make_async_copy(oo, oo_here, oo_sem)
    own_oo.start()

    def piece(at_z):
        return slab.at[:, g, at_z, pl.ds(pl.multiple_of(y * CHUNK, CHUNK), CHUNK)]

    own_slab = pltpu.make_async_copy(ov, piece(z), slab_sem)
    own_slab.start()
    load(0, 0).start()

    def turn(c):
        eight = oo_here[:, pl.ds(pl.multiple_of(c * CHUNK, CHUNK), CHUNK), :].astype(jnp.float32)
        oo_f32[:, 0:eight.shape[2]] = eight.reshape(nocc * CHUNK, eight.shape[2])
        for k in range(CHUNK):
            one = oo_f32[pl.ds(k, nocc, stride=CHUNK), :]
            oo_turned[k, :, 0:nocc] = one.T[0:I_ROWS, :].astype(jnp.bfloat16)

    own_oo.wait()
    oo_f32[...] = jnp.zeros_like(oo_f32)
    stage[...] = jnp.zeros_like(stage)
    turn(0)
    own_amps.wait()
    own_slab.wait()
    pl.semaphore_wait(barrier, len(order))

    def amps_copy(dg, b):
        here = gathered.at[g, :, pl.ds(b * BLOCK, widths[b])]
        return pltpu.make_async_remote_copy(
            src_ref=here,
            dst_ref=here,
            send_sem=amps_send.at[dg, b],
            recv_sem=amps_recv.at[dg, b],
            device_id=(lax.rem(g + dg, ng), v),
            device_id_type=MESH,
        )

    far_copy = pltpu.make_async_remote_copy(
        src_ref=piece(z),
        dst_ref=piece(z),
        send_sem=far_sems.at[0],
        recv_sem=far_sems.at[1],
        device_id=(g, z_far * inner + y),
        device_id_type=MESH,
    )

    def near_copy(dz, which):
        at_z = (z, z_far)[which]
        return pltpu.make_async_remote_copy(
            src_ref=piece(at_z),
            dst_ref=piece(at_z),
            send_sem=near_sems.at[0, which, dz],
            recv_sem=near_sems.at[1, which, dz],
            device_id=(g, ((z // half) * half + lax.rem(z + dz, half)) * inner + y),
            device_id_type=MESH,
        )

    def plane_copy(j):
        dg, dy = plane[j]
        column = slab.at[:, g, :, pl.ds(pl.multiple_of(y * CHUNK, CHUNK), CHUNK)]
        return pltpu.make_async_remote_copy(
            src_ref=column,
            dst_ref=column,
            send_sem=plane_send.at[j],
            recv_sem=plane_recv.at[j],
            device_id=(lax.rem(g + dg, ng), z * inner + lax.rem(y + dy, inner)),
            device_id_type=MESH,
        )

    for b in range(blocks):
        for dg in range(1, ng):
            amps_copy(dg, b).start()
    far_copy.start()
    load(0, edge).start()
    load(0, 0).wait()

    def put(k, value, add):
        at_rows = pl.ds(k * I_ROWS if isinstance(k, int) else pl.multiple_of(k * I_ROWS, I_ROWS), I_ROWS)
        for t in range(-(-value.shape[1] // LANES)):
            at, to = t * LANES, min(t * LANES + LANES, value.shape[1])
            if add:
                stage[t, at_rows, 0:to - at] += value[:, at:to]
            else:
                stage[t, at_rows, 0:to - at] = value[:, at:to]

    def hole(k, b):
        return lax.dot_general(
            oo_turned[k, :, 0:nocc], amps_all[:, b * BLOCK:b * BLOCK + widths[b]], (((1,), (0,)), ((), ())),
            preferred_element_type=jnp.float32,
        )

    for b in range(blocks):
        lo, hi = b * BLOCK, b * BLOCK + widths[b]
        for dg in range(1, ng):
            amps_copy(dg, b).wait_send()
            amps_copy(dg, b).wait_recv()
        for s in range(ng):
            rows_f32[s * held:(s + 1) * held, lo:hi] = gathered[s, :, lo:hi].astype(jnp.float32)
        amps_all[:, lo:hi] = rows_f32[0:ng * held, lo:hi].astype(jnp.bfloat16)

        for k in range(CHUNK):
            part = lax.dot_general(
                amps_all[0:I_ROWS, lo:hi], vv_slots[0, k, 0:widths[0], lo:hi], (((1,), (1,)), ((), ())),
                preferred_element_type=jnp.float32,
            )
            put(k, part - hole(k, 0) if b == 0 else part, b > 0)

    def owner(dv, dg):
        return lax.rem(g + dg, ng), lax.rem(v + nv + dv * (1 - 2 * lax.rem(g, 2)), nv)

    def dress(c, b, ready=False):
        width = widths[b]
        slot = slot_of(c, b)

        def compute():
            load(c, b).wait()

            @pl.loop(0, CHUNK)
            def _(k):
                direct = lax.dot_general(
                    amps_all[0:I_ROWS, :], vv_slots[slot, k, 0:width, :], (((1,), (1,)), ((), ())),
                    preferred_element_type=jnp.float32,
                )
                put(k, direct - hole(k, b), False)

        if not ready:
            compute()

        columns = pl.ds(0, full[b])
        landing = received.at[c, b, :, pl.ds(pl.multiple_of(me * CHUNK, CHUNK), CHUNK), columns]

        def regroup(to):
            first = to * per
            for i in range(per):
                for t in range(-(-width // LANES)):
                    rows = stage[t, pl.ds(first + i, CHUNK, stride=I_ROWS), :]
                    if t * LANES < full[b]:
                        dressed[c, b, first + i, :, t * LANES:t * LANES + LANES] = rows.astype(jnp.bfloat16)
                    else:
                        packed[to, c * per + i] = rows.astype(jnp.bfloat16)

        def send(step):
            to_g, to_v = owner(*step)
            pltpu.make_async_remote_copy(
                src_ref=dressed.at[c, b, pl.ds((to_g * nv + to_v) * per, per), :, columns],
                dst_ref=landing,
                send_sem=send_sem.at[b],
                recv_sem=recv_sem.at[c, b],
                device_id=(to_g, to_v),
                device_id_type=MESH,
            ).start()

        for at, step in enumerate(order):
            to_g, to_v = owner(*step)
            regroup(to_g * nv + to_v)
            if at >= 2:
                send(order[at - 2])
        regroup(me)
        send(order[-2])
        send(order[-1])
        pltpu.make_async_copy(
            dressed.at[c, b, pl.ds(me * per, per), :, columns], landing, own_sem.at[c, b]
        ).start()

        def ahead(holds, *args):
            @pl.when(holds)
            def _():
                load(*args).start()

        if ready:
            ahead(1 < chunks, 1, edge)
        elif b == edge:
            ahead(c + 2 < chunks, c + 2, edge)
            ahead(c + 2 == chunks, 0, 1)
            ahead(c + 1 == chunks, 0, 2)
        elif b + 2 < edge:
            load(c, b + 2).start()
        else:
            ahead(c + 1 < chunks, c + 1, b + 2 - edge)

    def lanes_from(lo):
        lane = lax.broadcasted_iota(jnp.int32, (CHUNK, LANES), 1)
        return (lane >= lo) & (lane < lo + ROWS)

    def pack(d):
        for j in range(kept):
            merged = packed[d, j].astype(jnp.float32)
            for slot in range(room):
                cell = slot * kept + j
                if cell < moved * cells:
                    u, p = cell // cells, cell % cells
                    lo = rest + slot * ROWS
                    turned = pltpu.roll(packed[d, kept + u].astype(jnp.float32), (lo - p * ROWS) % LANES, 1)
                    merged = jnp.where(lanes_from(lo), turned, merged)
            packed[d, j] = merged.astype(jnp.bfloat16)

    def unpack(d):
        for u in range(moved):
            whole = jnp.zeros((CHUNK, LANES), jnp.float32)
            for p in range(cells):
                slot, j = (u * cells + p) // kept, (u * cells + p) % kept
                lo = rest + slot * ROWS
                turned = pltpu.roll(unpacked[d, j].astype(jnp.float32), (p * ROWS - lo) % LANES, 1)
                whole = jnp.where(lanes_from(p * ROWS), turned, whole)
            unpacked[d, kept + u] = whole.astype(jnp.bfloat16)

    rest_landing = unpacked.at[me, pl.ds(0, kept)]
    own_rest = pltpu.make_async_copy(packed.at[me, pl.ds(0, kept)], rest_landing, rest_own)

    def send_rest():
        pl.loop(0, ng * nv)(pack)
        for step in order:
            to_g, to_v = owner(*step)
            pltpu.make_async_remote_copy(
                src_ref=packed.at[to_g * nv + to_v, pl.ds(0, kept)],
                dst_ref=rest_landing,
                send_sem=rest_send,
                recv_sem=rest_recv,
                device_id=(to_g, to_v),
                device_id_type=MESH,
            ).start()
        own_rest.start()

    dress(0, 0, True)

    @pl.loop(0, chunks)
    def _(c):
        turn(c)
        dress(c, edge)

        @pl.when(c == 0)
        def _():
            far_copy.wait_send()
            far_copy.wait_recv()
            for dz in range(1, half):
                near_copy(dz, 0).start()
                near_copy(dz, 1).start()

        @pl.when(c == 2)
        def _():
            for dz in range(1, half):
                for which in range(2):
                    near_copy(dz, which).wait_send()
                    near_copy(dz, which).wait_recv()
            for j in range(len(plane)):
                plane_copy(j).start()

    send_rest()

    @pl.loop(0, chunks)
    def _(c):
        turn(c)
        pl.when(c > 0)(functools.partial(dress, c, 0))
        for b in range(1, edge):
            dress(c, b)

    partial[...] = jnp.zeros_like(partial)
    for j in range(len(plane)):
        plane_copy(j).wait_send()
        plane_copy(j).wait_recv()

    def arrived(c, b):
        columns = pl.ds(0, full[b])
        others = received.at[c, b, :, pl.ds(0, depth - CHUNK), columns]
        pltpu.make_async_copy(others, others, recv_sem.at[c, b]).wait()
        mine = received.at[c, b, :, pl.ds(0, CHUNK), columns]
        pltpu.make_async_copy(mine, mine, own_sem.at[c, b]).wait()

    def add(i, first, lhs, rhs):
        rows = pl.ds(first, lhs.shape[1])
        for lo in range(0, slab.shape[-1], COLUMNS):
            partial[i, rows, lo:lo + COLUMNS] += lax.dot_general(
                lhs, rhs[:, lo:lo + COLUMNS], (((0,), (0,)), ((), ())),
                preferred_element_type=jnp.float32,
            )

    def contract_block(c, b):
        arrived(c, b)
        rhs = slab[c].reshape(depth, slab.shape[-1])

        @pl.loop(0, per)
        def _(i):
            add(i, b * BLOCK, received[c, b, i, :, 0:full[b]], rhs)

    contract_block(0, 0)

    @pl.loop(0, chunks)
    def _(c):
        contract_block(c, edge)

    others = unpacked.at[pl.ds(0, ng * nv - 1), pl.ds(0, kept)]
    pltpu.make_async_copy(others, others, rest_recv).wait()
    own_rest.wait()
    pl.loop(0, ng * nv)(unpack)

    @pl.loop(0, chunks)
    def _(c):
        rhs = slab[c].reshape(depth, slab.shape[-1])

        @pl.loop(0, per)
        def _(i):
            lhs = unpacked[:, c * per + i].reshape(depth, LANES)[:, 0:rest]
            add(i, nvirt - rest, lhs, rhs)

    @pl.loop(0, chunks)
    def _(c):
        pl.when(c > 0)(functools.partial(contract_block, c, 0))
        for b in range(1, edge - 1):
            contract_block(c, b)
        pl.when(c + 1 < chunks)(functools.partial(contract_block, c, edge - 1))

    arrived(chunks - 1, edge - 1)
    for b in range(blocks):
        sent = received.at[:, b, :, pl.ds(0, depth - CHUNK), pl.ds(0, full[b])]
        pltpu.make_async_copy(sent, sent, send_sem.at[b]).wait()
    pltpu.make_async_copy(others, others, rest_send).wait()


def finish_kernel(partial, received, slab, out, tail, sems):
    last, block = received.shape[0] - 1, received.shape[1] - 2
    per, nvirt = partial.shape[0], partial.shape[1]
    lo, hi = block * BLOCK, block * BLOCK + BLOCK
    copies = []

    def copy(src, dst):
        copies.append(pltpu.make_async_copy(src, dst, sems.at[len(copies)]))
        copies[-1].start()

    for i in range(per):
        copy(partial.at[i, 0:lo], out.at[i, 0:lo])
        copy(partial.at[i, hi:nvirt], out.at[i, hi:nvirt])
    rhs = slab[last].reshape(received.shape[3], slab.shape[-1])
    for i in range(per):
        tail[i] = partial[i, lo:hi, :] + lax.dot_general(
            received[last, block, i], rhs, (((0,), (0,)), ((), ())),
            preferred_element_type=jnp.float32,
        )
        copy(tail.at[i], out.at[i, lo:hi])
    for one in copies:
        one.wait()


def contract(ng, nv, vv_vectors, oo_vectors, ov_slab, amplitudes):
    local_count, nvirt = vv_vectors.shape[0], vv_vectors.shape[1]
    width = ov_slab.shape[1]
    devices = ng * nv
    inner = 2
    outer = nv // inner
    chunks = local_count // CHUNK
    blocks = -(-nvirt // BLOCK)
    per = I_ROWS // devices
    nocc = ng * amplitudes.shape[0]
    hbm = pl.BlockSpec(memory_space=pltpu.HBM)
    vmem = pl.BlockSpec(memory_space=pltpu.VMEM)
    dma = pltpu.SemaphoreType.DMA
    stay = functools.partial(pltpu.with_memory_space_constraint, memory_space=pltpu.HBM)
    partial, received, slab = pl.pallas_call(
        functools.partial(exchange_kernel, ng, nv, inner),
        out_shape=(
            jax.ShapeDtypeStruct((per, nvirt, width), jnp.float32),
            jax.ShapeDtypeStruct((chunks, blocks, per, devices * CHUNK, BLOCK), jnp.bfloat16),
            jax.ShapeDtypeStruct((chunks, ng, outer, inner * CHUNK, width), jnp.bfloat16),
        ),
        in_specs=[hbm, hbm, hbm, hbm],
        out_specs=(vmem, vmem, vmem),
        scratch_shapes=[
            pltpu.VMEM((devices, chunks * per, CHUNK, LANES), jnp.bfloat16),
            pltpu.VMEM((devices, chunks * per, CHUNK, LANES), jnp.bfloat16),
            pltpu.VMEM((blocks, CHUNK, BLOCK, nvirt), jnp.bfloat16),
            pltpu.VMEM((nocc, local_count, nocc), jnp.bfloat16),
            pltpu.VMEM((nocc * CHUNK, LANES), jnp.float32),
            pltpu.VMEM((CHUNK, I_ROWS, LANES), jnp.bfloat16),
            pltpu.VMEM((BLOCK // LANES, CHUNK * I_ROWS, LANES), jnp.float32),
            pltpu.VMEM((chunks, blocks, I_ROWS, CHUNK, BLOCK), jnp.bfloat16),
            pltpu.VMEM((ng,) + amplitudes.shape, jnp.bfloat16),
            pltpu.VMEM((nocc, nvirt), jnp.float32),
            pltpu.VMEM((nocc, nvirt), jnp.bfloat16),
            dma((blocks,)),
            dma((blocks,)),
            dma((chunks, blocks)),
            dma((chunks, blocks)),
            dma,
            dma((2,)),
            dma((2, 2, outer // 2)),
            dma((ng * inner - 1,)),
            dma((ng * inner - 1,)),
            dma,
            dma((ng, blocks)),
            dma((ng, blocks)),
            dma,
            dma,
            dma,
            dma,
        ],
        compiler_params=pltpu.CompilerParams(
            collective_id=0, has_side_effects=True, vmem_limit_bytes=LIMIT_MIB * 1024 * 1024
        ),
    )(
        stay(amplitudes), stay(jnp.transpose(oo_vectors, (1, 0, 2))),
        stay(ov_slab.reshape(chunks, CHUNK, width)), stay(vv_vectors),
    )
    return pl.pallas_call(
        finish_kernel,
        out_shape=jax.ShapeDtypeStruct((per, nvirt, width), jnp.float32),
        in_specs=[vmem, vmem, vmem],
        out_specs=hbm,
        scratch_shapes=[
            pltpu.VMEM((per, BLOCK, width), jnp.float32),
            dma((3 * per,)),
        ],
        compiler_params=pltpu.CompilerParams(vmem_limit_bytes=FINISH_MIB * 1024 * 1024),
    )(partial, received, slab).reshape(per * nvirt, width)


def plain(vv_vectors, oo_vectors, ov_slab, amps_all):
    local_count, nvirt = vv_vectors.shape[0], vv_vectors.shape[1]
    window = amps_all[:I_ROWS]
    direct_term = jnp.einsum("ib,pab->pia", window, vv_vectors, preferred_element_type=jnp.float32)
    hole_term = jnp.einsum(
        "pji,ja->pia", oo_vectors[:, :, :I_ROWS], amps_all, preferred_element_type=jnp.float32
    )
    dressed = (direct_term - hole_term).astype(jnp.bfloat16).reshape(local_count, I_ROWS * nvirt)
    regrouped = lax.all_to_all(dressed, ("grp", "vec"), split_axis=1, concat_axis=0, tiled=True)
    return lax.dot_general(
        regrouped,
        lax.all_gather(ov_slab, ("grp", "vec"), axis=0, tiled=True),
        (((0,), (0,)), ((), ())),
        preferred_element_type=jnp.float32,
    )


def solution(mesh):
    ng, nv = mesh.shape["grp"], mesh.shape["vec"]

    def shards(vv_vectors, oo_vectors, ov_slab, amplitudes):
        local_count, nvirt = vv_vectors.shape[0], vv_vectors.shape[1]
        fits = (
            I_ROWS % (ng * nv) == 0 and nv % 4 == 0 and local_count % CHUNK == 0 and nvirt % CHUNK == 0
            and LANES < nvirt % BLOCK < BLOCK
            and nvirt > 3 * BLOCK and local_count > 2 * CHUNK
            and oo_vectors.shape[1] <= LANES and ov_slab.shape[1] % COLUMNS == 0
        )
        if not fits:
            amps_all = lax.all_gather(amplitudes, "grp", axis=0, tiled=True)
            return plain(vv_vectors, oo_vectors, ov_slab, amps_all)
        return contract(ng, nv, vv_vectors, oo_vectors, ov_slab, amplitudes)

    return jax.shard_map(
        shards,
        mesh=mesh,
        in_specs=(
            P(("grp", "vec"), None, None),
            P(("grp", "vec"), None, None),
            P(("grp", "vec"), None),
            P("grp", None),
        ),
        out_specs=P(("grp", "vec"), None),
        check_vma=False,
    )
```

```python
import functools
import jax
import jax.numpy as jnp
from jax import lax
from jax.experimental import pallas as pl
from jax.experimental.pallas import tpu as pltpu
from jax.sharding import PartitionSpec as P

I_ROWS = 96
CHUNK = 8
BLOCK = 256
LANES = 128
ROWS = 8
COLUMNS = 256
LIMIT_MIB = 30
FINISH_MIB = 8
MESH = pl.DeviceIdType.MESH


def farthest_first(count):
    return sorted(range(count), key=lambda k: (abs(k - count // 2), k))


def packing(total, nvirt):
    rest = nvirt % LANES
    cells, room = rest // ROWS, (LANES - rest) // ROWS
    kept = -(-total * cells // (cells + room))
    return rest, cells, room, kept


def exchange_kernel(
    ng, nv, inner, amps, oo, ov, vv, partial, received, slab,
    packed, unpacked, vv_slots, oo_here, oo_f32, oo_turned, stage, dressed, gathered, rows_f32, amps_all,
    vv_sem, send_sem, recv_sem, own_sem, oo_sem, far_sems, near_sems, plane_send, plane_recv, slab_sem,
    amps_send, amps_recv, amps_own, rest_send, rest_recv, rest_own,
):
    g = lax.axis_index("grp")
    v = lax.axis_index("vec")
    me = g * nv + v
    local_count, nvirt = vv.shape[0], vv.shape[1]
    nocc = oo.shape[0]
    chunks = local_count // CHUNK
    blocks = -(-nvirt // BLOCK)
    widths = [min(BLOCK, nvirt - b * BLOCK) for b in range(blocks)]
    per = I_ROWS // (ng * nv)
    edge = blocks - 1
    slots = vv_slots.shape[0]
    rest, cells, room, kept = packing(chunks * per, nvirt)
    moved = chunks * per - kept
    full = [w // LANES * LANES for w in widths]
    depth = ng * nv * CHUNK
    outer = nv // inner
    half = outer // 2
    z = v // inner
    y = lax.rem(v, inner)
    z_far = lax.rem(z + half, outer)
    held = amps.shape[0]
    order = [(dv, dg) for dv in farthest_first(nv) for dg in farthest_first(ng) if (dg, dv) != (0, 0)]
    plane = [(dg, dy) for dg in range(ng) for dy in range(inner) if (dg, dy) != (0, 0)]

    def slot_of(c, b):
        if b == edge:
            return lax.rem(c + 1, slots)
        if b == 0:
            return lax.rem(jnp.where(c == 0, 0, chunks + edge * c), slots)
        return lax.rem(chunks + edge * c + b, slots)

    def load(c, b):
        return pltpu.make_async_copy(
            vv.at[pl.ds(pl.multiple_of(c * CHUNK, CHUNK), CHUNK), pl.ds(b * BLOCK, widths[b])],
            vv_slots.at[slot_of(c, b), :, pl.ds(0, widths[b])],
            vv_sem.at[slot_of(c, b)],
        )

    barrier = pltpu.get_barrier_semaphore()
    for dv, dg in order:
        pl.semaphore_signal(
            barrier, inc=1, device_id=(lax.rem(g + dg, ng), lax.rem(v + dv, nv)), device_id_type=MESH
        )
    own_amps = pltpu.make_async_copy(amps, gathered.at[g], amps_own)
    own_amps.start()
    own_oo = pltpu.make_async_copy(oo, oo_here, oo_sem)
    own_oo.start()

    def piece(at_z):
        return slab.at[:, g, at_z, pl.ds(pl.multiple_of(y * CHUNK, CHUNK), CHUNK)]

    own_slab = pltpu.make_async_copy(ov, piece(z), slab_sem)
    own_slab.start()
    load(0, 0).start()

    def turn(c):
        eight = oo_here[:, pl.ds(pl.multiple_of(c * CHUNK, CHUNK), CHUNK), :].astype(jnp.float32)
        oo_f32[:, 0:eight.shape[2]] = eight.reshape(nocc * CHUNK, eight.shape[2])
        for k in range(CHUNK):
            one = oo_f32[pl.ds(k, nocc, stride=CHUNK), :]
            oo_turned[k, :, 0:nocc] = one.T[0:I_ROWS, :].astype(jnp.bfloat16)

    own_oo.wait()
    oo_f32[...] = jnp.zeros_like(oo_f32)
    stage[...] = jnp.zeros_like(stage)
    turn(0)
    own_amps.wait()
    own_slab.wait()
    pl.semaphore_wait(barrier, len(order))

    def amps_copy(dg, b):
        here = gathered.at[g, :, pl.ds(b * BLOCK, widths[b])]
        return pltpu.make_async_remote_copy(
            src_ref=here,
            dst_ref=here,
            send_sem=amps_send.at[dg, b],
            recv_sem=amps_recv.at[dg, b],
            device_id=(lax.rem(g + dg, ng), v),
            device_id_type=MESH,
        )

    far_copy = pltpu.make_async_remote_copy(
        src_ref=piece(z),
        dst_ref=piece(z),
        send_sem=far_sems.at[0],
        recv_sem=far_sems.at[1],
        device_id=(g, z_far * inner + y),
        device_id_type=MESH,
    )

    def near_copy(dz, which):
        at_z = (z, z_far)[which]
        return pltpu.make_async_remote_copy(
            src_ref=piece(at_z),
            dst_ref=piece(at_z),
            send_sem=near_sems.at[0, which, dz],
            recv_sem=near_sems.at[1, which, dz],
            device_id=(g, ((z // half) * half + lax.rem(z + dz, half)) * inner + y),
            device_id_type=MESH,
        )

    def plane_copy(j):
        dg, dy = plane[j]
        column = slab.at[:, g, :, pl.ds(pl.multiple_of(y * CHUNK, CHUNK), CHUNK)]
        return pltpu.make_async_remote_copy(
            src_ref=column,
            dst_ref=column,
            send_sem=plane_send.at[j],
            recv_sem=plane_recv.at[j],
            device_id=(lax.rem(g + dg, ng), z * inner + lax.rem(y + dy, inner)),
            device_id_type=MESH,
        )

    for b in range(blocks):
        for dg in range(1, ng):
            amps_copy(dg, b).start()
    far_copy.start()
    load(0, 0).wait()

    def put(k, value, add):
        at_rows = pl.ds(k * I_ROWS if isinstance(k, int) else pl.multiple_of(k * I_ROWS, I_ROWS), I_ROWS)
        for t in range(-(-value.shape[1] // LANES)):
            at, to = t * LANES, min(t * LANES + LANES, value.shape[1])
            if add:
                stage[t, at_rows, 0:to - at] += value[:, at:to]
            else:
                stage[t, at_rows, 0:to - at] = value[:, at:to]

    def hole(k, b):
        return lax.dot_general(
            oo_turned[k, :, 0:nocc], amps_all[:, b * BLOCK:b * BLOCK + widths[b]], (((1,), (0,)), ((), ())),
            preferred_element_type=jnp.float32,
        )

    for b in range(blocks):
        lo, hi = b * BLOCK, b * BLOCK + widths[b]
        for dg in range(1, ng):
            amps_copy(dg, b).wait_send()
            amps_copy(dg, b).wait_recv()
        for s in range(ng):
            rows_f32[s * held:(s + 1) * held, lo:hi] = gathered[s, :, lo:hi].astype(jnp.float32)
        amps_all[:, lo:hi] = rows_f32[0:ng * held, lo:hi].astype(jnp.bfloat16)

        for k in range(CHUNK):
            part = lax.dot_general(
                amps_all[0:I_ROWS, lo:hi], vv_slots[0, k, 0:widths[0], lo:hi], (((1,), (1,)), ((), ())),
                preferred_element_type=jnp.float32,
            )
            put(k, part - hole(k, 0) if b == 0 else part, b > 0)

    def owner(dv, dg):
        return lax.rem(g + dg, ng), lax.rem(v + nv + dv * (1 - 2 * lax.rem(g, 2)), nv)

    def dress(c, b, ready=False):
        width = widths[b]
        slot = slot_of(c, b)

        def compute():
            load(c, b).wait()

            @pl.loop(0, CHUNK)
            def _(k):
                direct = lax.dot_general(
                    amps_all[0:I_ROWS, :], vv_slots[slot, k, 0:width, :], (((1,), (1,)), ((), ())),
                    preferred_element_type=jnp.float32,
                )
                put(k, direct - hole(k, b), False)

        if not ready:
            compute()

        columns = pl.ds(0, full[b])
        landing = received.at[c, b, :, pl.ds(pl.multiple_of(me * CHUNK, CHUNK), CHUNK), columns]

        def regroup(to):
            first = to * per
            for i in range(per):
                for t in range(-(-width // LANES)):
                    rows = stage[t, pl.ds(first + i, CHUNK, stride=I_ROWS), :]
                    if t * LANES < full[b]:
                        dressed[c, b, first + i, :, t * LANES:t * LANES + LANES] = rows.astype(jnp.bfloat16)
                    else:
                        packed[to, c * per + i] = rows.astype(jnp.bfloat16)

        def send(step):
            to_g, to_v = owner(*step)
            pltpu.make_async_remote_copy(
                src_ref=dressed.at[c, b, pl.ds((to_g * nv + to_v) * per, per), :, columns],
                dst_ref=landing,
                send_sem=send_sem.at[b],
                recv_sem=recv_sem.at[c, b],
                device_id=(to_g, to_v),
                device_id_type=MESH,
            ).start()

        for at, step in enumerate(order):
            to_g, to_v = owner(*step)
            regroup(to_g * nv + to_v)
            if at >= 2:
                send(order[at - 2])
        regroup(me)
        send(order[-2])
        send(order[-1])
        pltpu.make_async_copy(
            dressed.at[c, b, pl.ds(me * per, per), :, columns], landing, own_sem.at[c, b]
        ).start()

        def ahead(holds, *args):
            @pl.when(holds)
            def _():
                load(*args).start()

        if ready:
            ahead(1 < chunks, 1, edge)
        elif b == edge:
            ahead(c + 2 < chunks, c + 2, edge)
            ahead(c + 2 == chunks, 0, 1)
            ahead(c + 1 == chunks, 0, 2)
        elif b + 2 < edge:
            load(c, b + 2).start()
        else:
            ahead(c + 1 < chunks, c + 1, b + 2 - edge)

    def lanes_from(lo):
        lane = lax.broadcasted_iota(jnp.int32, (CHUNK, LANES), 1)
        return (lane >= lo) & (lane < lo + ROWS)

    def pack(d):
        for j in range(kept):
            merged = packed[d, j].astype(jnp.float32)
            for slot in range(room):
                cell = slot * kept + j
                if cell < moved * cells:
                    u, p = cell // cells, cell % cells
                    lo = rest + slot * ROWS
                    turned = pltpu.roll(packed[d, kept + u].astype(jnp.float32), (lo - p * ROWS) % LANES, 1)
                    merged = jnp.where(lanes_from(lo), turned, merged)
            packed[d, j] = merged.astype(jnp.bfloat16)

    def unpack(d):
        for u in range(moved):
            whole = jnp.zeros((CHUNK, LANES), jnp.float32)
            for p in range(cells):
                slot, j = (u * cells + p) // kept, (u * cells + p) % kept
                lo = rest + slot * ROWS
                turned = pltpu.roll(unpacked[d, j].astype(jnp.float32), (p * ROWS - lo) % LANES, 1)
                whole = jnp.where(lanes_from(p * ROWS), turned, whole)
            unpacked[d, kept + u] = whole.astype(jnp.bfloat16)

    rest_landing = unpacked.at[me, pl.ds(0, kept)]
    own_rest = pltpu.make_async_copy(packed.at[me, pl.ds(0, kept)], rest_landing, rest_own)

    def send_rest():
        pl.loop(0, ng * nv)(pack)
        for step in order:
            to_g, to_v = owner(*step)
            pltpu.make_async_remote_copy(
                src_ref=packed.at[to_g * nv + to_v, pl.ds(0, kept)],
                dst_ref=rest_landing,
                send_sem=rest_send,
                recv_sem=rest_recv,
                device_id=(to_g, to_v),
                device_id_type=MESH,
            ).start()
        own_rest.start()

    load(0, edge).start()
    dress(0, 0, True)

    @pl.loop(0, chunks)
    def _(c):
        turn(c)
        dress(c, edge)

        @pl.when(c == 0)
        def _():
            far_copy.wait_send()
            far_copy.wait_recv()
            for dz in range(1, half):
                near_copy(dz, 0).start()
                near_copy(dz, 1).start()

        @pl.when(c == 2)
        def _():
            for dz in range(1, half):
                for which in range(2):
                    near_copy(dz, which).wait_send()
                    near_copy(dz, which).wait_recv()
            for j in range(len(plane)):
                plane_copy(j).start()

    send_rest()

    @pl.loop(0, chunks)
    def _(c):
        turn(c)
        pl.when(c > 0)(functools.partial(dress, c, 0))
        for b in range(1, edge):
            dress(c, b)

    partial[...] = jnp.zeros_like(partial)
    for j in range(len(plane)):
        plane_copy(j).wait_send()
        plane_copy(j).wait_recv()

    def arrived(c, b):
        columns = pl.ds(0, full[b])
        others = received.at[c, b, :, pl.ds(0, depth - CHUNK), columns]
        pltpu.make_async_copy(others, others, recv_sem.at[c, b]).wait()
        mine = received.at[c, b, :, pl.ds(0, CHUNK), columns]
        pltpu.make_async_copy(mine, mine, own_sem.at[c, b]).wait()

    def add(i, first, lhs, rhs):
        rows = pl.ds(first, lhs.shape[1])
        for lo in range(0, slab.shape[-1], COLUMNS):
            partial[i, rows, lo:lo + COLUMNS] += lax.dot_general(
                lhs, rhs[:, lo:lo + COLUMNS], (((0,), (0,)), ((), ())),
                preferred_element_type=jnp.float32,
            )

    def contract_block(c, b):
        arrived(c, b)
        rhs = slab[c].reshape(depth, slab.shape[-1])

        @pl.loop(0, per)
        def _(i):
            add(i, b * BLOCK, received[c, b, i, :, 0:full[b]], rhs)

    contract_block(0, 0)

    @pl.loop(0, chunks)
    def _(c):
        contract_block(c, edge)

    others = unpacked.at[pl.ds(0, ng * nv - 1), pl.ds(0, kept)]
    pltpu.make_async_copy(others, others, rest_recv).wait()
    own_rest.wait()
    pl.loop(0, ng * nv)(unpack)

    @pl.loop(0, chunks)
    def _(c):
        rhs = slab[c].reshape(depth, slab.shape[-1])

        @pl.loop(0, per)
        def _(i):
            lhs = unpacked[:, c * per + i].reshape(depth, LANES)[:, 0:rest]
            add(i, nvirt - rest, lhs, rhs)

    @pl.loop(0, chunks)
    def _(c):
        pl.when(c > 0)(functools.partial(contract_block, c, 0))
        for b in range(1, edge - 1):
            contract_block(c, b)
        pl.when(c + 1 < chunks)(functools.partial(contract_block, c, edge - 1))

    arrived(chunks - 1, edge - 1)
    for b in range(blocks):
        sent = received.at[:, b, :, pl.ds(0, depth - CHUNK), pl.ds(0, full[b])]
        pltpu.make_async_copy(sent, sent, send_sem.at[b]).wait()
    pltpu.make_async_copy(others, others, rest_send).wait()


def finish_kernel(partial, received, slab, out, tail, sems):
    last, block = received.shape[0] - 1, received.shape[1] - 2
    per, nvirt = partial.shape[0], partial.shape[1]
    lo, hi = block * BLOCK, block * BLOCK + BLOCK
    copies = []

    def copy(src, dst):
        copies.append(pltpu.make_async_copy(src, dst, sems.at[len(copies)]))
        copies[-1].start()

    for i in range(per):
        copy(partial.at[i, 0:lo], out.at[i, 0:lo])
        copy(partial.at[i, hi:nvirt], out.at[i, hi:nvirt])
    rhs = slab[last].reshape(received.shape[3], slab.shape[-1])
    for i in range(per):
        tail[i] = partial[i, lo:hi, :] + lax.dot_general(
            received[last, block, i], rhs, (((0,), (0,)), ((), ())),
            preferred_element_type=jnp.float32,
        )
        copy(tail.at[i], out.at[i, lo:hi])
    for one in copies:
        one.wait()


def contract(ng, nv, vv_vectors, oo_vectors, ov_slab, amplitudes):
    local_count, nvirt = vv_vectors.shape[0], vv_vectors.shape[1]
    width = ov_slab.shape[1]
    devices = ng * nv
    inner = 2
    outer = nv // inner
    chunks = local_count // CHUNK
    blocks = -(-nvirt // BLOCK)
    per = I_ROWS // devices
    nocc = ng * amplitudes.shape[0]
    hbm = pl.BlockSpec(memory_space=pltpu.HBM)
    vmem = pl.BlockSpec(memory_space=pltpu.VMEM)
    dma = pltpu.SemaphoreType.DMA
    stay = functools.partial(pltpu.with_memory_space_constraint, memory_space=pltpu.HBM)
    partial, received, slab = pl.pallas_call(
        functools.partial(exchange_kernel, ng, nv, inner),
        out_shape=(
            jax.ShapeDtypeStruct((per, nvirt, width), jnp.float32),
            jax.ShapeDtypeStruct((chunks, blocks, per, devices * CHUNK, BLOCK), jnp.bfloat16),
            jax.ShapeDtypeStruct((chunks, ng, outer, inner * CHUNK, width), jnp.bfloat16),
        ),
        in_specs=[hbm, hbm, hbm, hbm],
        out_specs=(vmem, vmem, vmem),
        scratch_shapes=[
            pltpu.VMEM((devices, chunks * per, CHUNK, LANES), jnp.bfloat16),
            pltpu.VMEM((devices, chunks * per, CHUNK, LANES), jnp.bfloat16),
            pltpu.VMEM((blocks, CHUNK, BLOCK, nvirt), jnp.bfloat16),
            pltpu.VMEM((nocc, local_count, nocc), jnp.bfloat16),
            pltpu.VMEM((nocc * CHUNK, LANES), jnp.float32),
            pltpu.VMEM((CHUNK, I_ROWS, LANES), jnp.bfloat16),
            pltpu.VMEM((BLOCK // LANES, CHUNK * I_ROWS, LANES), jnp.float32),
            pltpu.VMEM((chunks, blocks, I_ROWS, CHUNK, BLOCK), jnp.bfloat16),
            pltpu.VMEM((ng,) + amplitudes.shape, jnp.bfloat16),
            pltpu.VMEM((nocc, nvirt), jnp.float32),
            pltpu.VMEM((nocc, nvirt), jnp.bfloat16),
            dma((blocks,)),
            dma((blocks,)),
            dma((chunks, blocks)),
            dma((chunks, blocks)),
            dma,
            dma((2,)),
            dma((2, 2, outer // 2)),
            dma((ng * inner - 1,)),
            dma((ng * inner - 1,)),
            dma,
            dma((ng, blocks)),
            dma((ng, blocks)),
            dma,
            dma,
            dma,
            dma,
        ],
        compiler_params=pltpu.CompilerParams(
            collective_id=0, has_side_effects=True, vmem_limit_bytes=LIMIT_MIB * 1024 * 1024
        ),
    )(
        stay(amplitudes), stay(jnp.transpose(oo_vectors, (1, 0, 2))),
        stay(ov_slab.reshape(chunks, CHUNK, width)), stay(vv_vectors),
    )
    return pl.pallas_call(
        finish_kernel,
        out_shape=jax.ShapeDtypeStruct((per, nvirt, width), jnp.float32),
        in_specs=[vmem, vmem, vmem],
        out_specs=hbm,
        scratch_shapes=[
            pltpu.VMEM((per, BLOCK, width), jnp.float32),
            dma((3 * per,)),
        ],
        compiler_params=pltpu.CompilerParams(vmem_limit_bytes=FINISH_MIB * 1024 * 1024),
    )(partial, received, slab).reshape(per * nvirt, width)


def plain(vv_vectors, oo_vectors, ov_slab, amps_all):
    local_count, nvirt = vv_vectors.shape[0], vv_vectors.shape[1]
    window = amps_all[:I_ROWS]
    direct_term = jnp.einsum("ib,pab->pia", window, vv_vectors, preferred_element_type=jnp.float32)
    hole_term = jnp.einsum(
        "pji,ja->pia", oo_vectors[:, :, :I_ROWS], amps_all, preferred_element_type=jnp.float32
    )
    dressed = (direct_term - hole_term).astype(jnp.bfloat16).reshape(local_count, I_ROWS * nvirt)
    regrouped = lax.all_to_all(dressed, ("grp", "vec"), split_axis=1, concat_axis=0, tiled=True)
    return lax.dot_general(
        regrouped,
        lax.all_gather(ov_slab, ("grp", "vec"), axis=0, tiled=True),
        (((0,), (0,)), ((), ())),
        preferred_element_type=jnp.float32,
    )


def solution(mesh):
    ng, nv = mesh.shape["grp"], mesh.shape["vec"]

    def shards(vv_vectors, oo_vectors, ov_slab, amplitudes):
        local_count, nvirt = vv_vectors.shape[0], vv_vectors.shape[1]
        fits = (
            I_ROWS % (ng * nv) == 0 and nv % 4 == 0 and local_count % CHUNK == 0 and nvirt % CHUNK == 0
            and LANES < nvirt % BLOCK < BLOCK
            and nvirt > 3 * BLOCK and local_count > 2 * CHUNK
            and oo_vectors.shape[1] <= LANES and ov_slab.shape[1] % COLUMNS == 0
        )
        if not fits:
            amps_all = lax.all_gather(amplitudes, "grp", axis=0, tiled=True)
            return plain(vv_vectors, oo_vectors, ov_slab, amps_all)
        return contract(ng, nv, vv_vectors, oo_vectors, ov_slab, amplitudes)

    return jax.shard_map(
        shards,
        mesh=mesh,
        in_specs=(
            P(("grp", "vec"), None, None),
            P(("grp", "vec"), None, None),
            P(("grp", "vec"), None),
            P("grp", None),
        ),
        out_specs=P(("grp", "vec"), None),
        check_vma=False,
    )
```

```python
import functools
import jax
import jax.numpy as jnp
from jax import lax
from jax.experimental import pallas as pl
from jax.experimental.pallas import tpu as pltpu
from jax.sharding import PartitionSpec as P

I_ROWS = 96
CHUNK = 8
BLOCK = 256
LANES = 128
ROWS = 8
COLUMNS = 256
LIMIT_MIB = 30
FINISH_MIB = 8
MESH = pl.DeviceIdType.MESH


def farthest_first(count):
    return sorted(range(count), key=lambda k: (abs(k - count // 2), k))


def packing(total, nvirt):
    rest = nvirt % LANES
    cells, room = rest // ROWS, (LANES - rest) // ROWS
    kept = -(-total * cells // (cells + room))
    return rest, cells, room, kept


def exchange_kernel(
    ng, nv, inner, amps, oo, ov, vv, partial, received, slab,
    packed, unpacked, vv_slots, oo_here, oo_f32, oo_turned, stage, dressed, gathered, rows_f32, amps_all,
    vv_sem, send_sem, recv_sem, own_sem, oo_sem, far_sems, near_sems, plane_send, plane_recv, slab_sem,
    amps_send, amps_recv, amps_own, rest_send, rest_recv, rest_own,
):
    g = lax.axis_index("grp")
    v = lax.axis_index("vec")
    me = g * nv + v
    local_count, nvirt = vv.shape[0], vv.shape[1]
    nocc = oo.shape[0]
    chunks = local_count // CHUNK
    blocks = -(-nvirt // BLOCK)
    widths = [min(BLOCK, nvirt - b * BLOCK) for b in range(blocks)]
    per = I_ROWS // (ng * nv)
    edge = blocks - 1
    slots = vv_slots.shape[0]
    rest, cells, room, kept = packing(chunks * per, nvirt)
    moved = chunks * per - kept
    full = [w // LANES * LANES for w in widths]
    depth = ng * nv * CHUNK
    outer = nv // inner
    half = outer // 2
    z = v // inner
    y = lax.rem(v, inner)
    z_far = lax.rem(z + half, outer)
    held = amps.shape[0]
    order = [(dv, dg) for dv in farthest_first(nv) for dg in range(ng) if (dg, dv) != (0, 0)]
    plane = [(dg, dy) for dg in range(ng) for dy in range(inner) if (dg, dy) != (0, 0)]

    def slot_of(c, b):
        if b == edge:
            return lax.rem(c + 1, slots)
        if b == 0:
            return lax.rem(jnp.where(c == 0, 0, chunks + edge * c), slots)
        return lax.rem(chunks + edge * c + b, slots)

    def load(c, b):
        return pltpu.make_async_copy(
            vv.at[pl.ds(pl.multiple_of(c * CHUNK, CHUNK), CHUNK), pl.ds(b * BLOCK, widths[b])],
            vv_slots.at[slot_of(c, b), :, pl.ds(0, widths[b])],
            vv_sem.at[slot_of(c, b)],
        )

    barrier = pltpu.get_barrier_semaphore()
    for dv, dg in order:
        pl.semaphore_signal(
            barrier, inc=1, device_id=(lax.rem(g + dg, ng), lax.rem(v + dv, nv)), device_id_type=MESH
        )
    own_amps = pltpu.make_async_copy(amps, gathered.at[g], amps_own)
    own_amps.start()
    own_oo = pltpu.make_async_copy(oo, oo_here, oo_sem)
    own_oo.start()

    def piece(at_z):
        return slab.at[:, g, at_z, pl.ds(pl.multiple_of(y * CHUNK, CHUNK), CHUNK)]

    own_slab = pltpu.make_async_copy(ov, piece(z), slab_sem)
    own_slab.start()
    load(0, 0).start()

    def turn(c):
        eight = oo_here[:, pl.ds(pl.multiple_of(c * CHUNK, CHUNK), CHUNK), :].astype(jnp.float32)
        oo_f32[:, 0:eight.shape[2]] = eight.reshape(nocc * CHUNK, eight.shape[2])
        for k in range(CHUNK):
            one = oo_f32[pl.ds(k, nocc, stride=CHUNK), :]
            oo_turned[k, :, 0:nocc] = one.T[0:I_ROWS, :].astype(jnp.bfloat16)

    own_oo.wait()
    oo_f32[...] = jnp.zeros_like(oo_f32)
    stage[...] = jnp.zeros_like(stage)
    turn(0)
    own_amps.wait()
    own_slab.wait()
    pl.semaphore_wait(barrier, len(order))

    def amps_copy(dg, b):
        here = gathered.at[g, :, pl.ds(b * BLOCK, widths[b])]
        return pltpu.make_async_remote_copy(
            src_ref=here,
            dst_ref=here,
            send_sem=amps_send.at[dg, b],
            recv_sem=amps_recv.at[dg, b],
            device_id=(lax.rem(g + dg, ng), v),
            device_id_type=MESH,
        )

    far_copy = pltpu.make_async_remote_copy(
        src_ref=piece(z),
        dst_ref=piece(z),
        send_sem=far_sems.at[0],
        recv_sem=far_sems.at[1],
        device_id=(g, z_far * inner + y),
        device_id_type=MESH,
    )

    def near_copy(dz, which):
        at_z = (z, z_far)[which]
        return pltpu.make_async_remote_copy(
            src_ref=piece(at_z),
            dst_ref=piece(at_z),
            send_sem=near_sems.at[0, which, dz],
            recv_sem=near_sems.at[1, which, dz],
            device_id=(g, ((z // half) * half + lax.rem(z + dz, half)) * inner + y),
            device_id_type=MESH,
        )

    def plane_copy(j):
        dg, dy = plane[j]
        column = slab.at[:, g, :, pl.ds(pl.multiple_of(y * CHUNK, CHUNK), CHUNK)]
        return pltpu.make_async_remote_copy(
            src_ref=column,
            dst_ref=column,
            send_sem=plane_send.at[j],
            recv_sem=plane_recv.at[j],
            device_id=(lax.rem(g + dg, ng), z * inner + lax.rem(y + dy, inner)),
            device_id_type=MESH,
        )

    far_copy.start()
    for b in range(blocks):
        for dg in range(1, ng):
            amps_copy(dg, b).start()
    load(0, 0).wait()

    def put(k, value, add):
        at_rows = pl.ds(k * I_ROWS if isinstance(k, int) else pl.multiple_of(k * I_ROWS, I_ROWS), I_ROWS)
        for t in range(-(-value.shape[1] // LANES)):
            at, to = t * LANES, min(t * LANES + LANES, value.shape[1])
            if add:
                stage[t, at_rows, 0:to - at] += value[:, at:to]
            else:
                stage[t, at_rows, 0:to - at] = value[:, at:to]

    def hole(k, b):
        return lax.dot_general(
            oo_turned[k, :, 0:nocc], amps_all[:, b * BLOCK:b * BLOCK + widths[b]], (((1,), (0,)), ((), ())),
            preferred_element_type=jnp.float32,
        )

    for b in range(blocks):
        lo, hi = b * BLOCK, b * BLOCK + widths[b]
        for dg in range(1, ng):
            amps_copy(dg, b).wait_recv()
        for s in range(ng):
            rows_f32[s * held:(s + 1) * held, lo:hi] = gathered[s, :, lo:hi].astype(jnp.float32)
        amps_all[:, lo:hi] = rows_f32[0:ng * held, lo:hi].astype(jnp.bfloat16)

        for k in range(CHUNK):
            part = lax.dot_general(
                amps_all[0:I_ROWS, lo:hi], vv_slots[0, k, 0:widths[0], lo:hi], (((1,), (1,)), ((), ())),
                preferred_element_type=jnp.float32,
            )
            put(k, part - hole(k, 0) if b == 0 else part, b > 0)

    def owner(dv, dg):
        return lax.rem(g + dg, ng), lax.rem(v + nv + dv * (1 - 2 * lax.rem(g, 2)), nv)

    def dress(c, b, ready=False):
        width = widths[b]
        slot = slot_of(c, b)

        def compute():
            load(c, b).wait()

            @pl.loop(0, CHUNK)
            def _(k):
                direct = lax.dot_general(
                    amps_all[0:I_ROWS, :], vv_slots[slot, k, 0:width, :], (((1,), (1,)), ((), ())),
                    preferred_element_type=jnp.float32,
                )
                put(k, direct - hole(k, b), False)

        if not ready:
            compute()

        columns = pl.ds(0, full[b])
        landing = received.at[c, b, :, pl.ds(pl.multiple_of(me * CHUNK, CHUNK), CHUNK), columns]

        def regroup(to):
            first = to * per
            for i in range(per):
                for t in range(-(-width // LANES)):
                    rows = stage[t, pl.ds(first + i, CHUNK, stride=I_ROWS), :]
                    if t * LANES < full[b]:
                        dressed[c, b, first + i, :, t * LANES:t * LANES + LANES] = rows.astype(jnp.bfloat16)
                    else:
                        packed[to, c * per + i] = rows.astype(jnp.bfloat16)

        def send(step):
            to_g, to_v = owner(*step)
            pltpu.make_async_remote_copy(
                src_ref=dressed.at[c, b, pl.ds((to_g * nv + to_v) * per, per), :, columns],
                dst_ref=landing,
                send_sem=send_sem.at[b],
                recv_sem=recv_sem.at[c, b],
                device_id=(to_g, to_v),
                device_id_type=MESH,
            ).start()

        for at, step in enumerate(order):
            to_g, to_v = owner(*step)
            regroup(to_g * nv + to_v)
            if at >= 2:
                send(order[at - 2])
        regroup(me)
        send(order[-2])
        send(order[-1])
        pltpu.make_async_copy(
            dressed.at[c, b, pl.ds(me * per, per), :, columns], landing, own_sem.at[c, b]
        ).start()

        def ahead(holds, *args):
            @pl.when(holds)
            def _():
                load(*args).start()

        if ready:
            ahead(1 < chunks, 1, edge)
        elif b == edge:
            ahead(c + 2 < chunks, c + 2, edge)
            ahead(c + 2 == chunks, 0, 1)
            ahead(c + 1 == chunks, 0, 2)
        elif b + 2 < edge:
            load(c, b + 2).start()
        else:
            ahead(c + 1 < chunks, c + 1, b + 2 - edge)

    def lanes_from(lo):
        lane = lax.broadcasted_iota(jnp.int32, (CHUNK, LANES), 1)
        return (lane >= lo) & (lane < lo + ROWS)

    def pack(d):
        for j in range(kept):
            merged = packed[d, j].astype(jnp.float32)
            for slot in range(room):
                cell = slot * kept + j
                if cell < moved * cells:
                    u, p = cell // cells, cell % cells
                    lo = rest + slot * ROWS
                    turned = pltpu.roll(packed[d, kept + u].astype(jnp.float32), (lo - p * ROWS) % LANES, 1)
                    merged = jnp.where(lanes_from(lo), turned, merged)
            packed[d, j] = merged.astype(jnp.bfloat16)

    def unpack(d):
        for u in range(moved):
            whole = jnp.zeros((CHUNK, LANES), jnp.float32)
            for p in range(cells):
                slot, j = (u * cells + p) // kept, (u * cells + p) % kept
                lo = rest + slot * ROWS
                turned = pltpu.roll(unpacked[d, j].astype(jnp.float32), (p * ROWS - lo) % LANES, 1)
                whole = jnp.where(lanes_from(p * ROWS), turned, whole)
            unpacked[d, kept + u] = whole.astype(jnp.bfloat16)

    rest_landing = unpacked.at[me, pl.ds(0, kept)]
    own_rest = pltpu.make_async_copy(packed.at[me, pl.ds(0, kept)], rest_landing, rest_own)

    def send_rest():
        pl.loop(0, ng * nv)(pack)
        for step in order:
            to_g, to_v = owner(*step)
            pltpu.make_async_remote_copy(
                src_ref=packed.at[to_g * nv + to_v, pl.ds(0, kept)],
                dst_ref=rest_landing,
                send_sem=rest_send,
                recv_sem=rest_recv,
                device_id=(to_g, to_v),
                device_id_type=MESH,
            ).start()
        own_rest.start()

    load(0, edge).start()
    dress(0, 0, True)
    for b in range(blocks):
        for dg in range(1, ng):
            amps_copy(dg, b).wait_send()

    @pl.loop(0, chunks)
    def _(c):
        turn(c)
        dress(c, edge)

        @pl.when(c == 0)
        def _():
            far_copy.wait_send()
            far_copy.wait_recv()
            for dz in range(1, half):
                near_copy(dz, 0).start()
                near_copy(dz, 1).start()

        @pl.when(c == 2)
        def _():
            for dz in range(1, half):
                for which in range(2):
                    near_copy(dz, which).wait_send()
                    near_copy(dz, which).wait_recv()
            for j in range(len(plane)):
                plane_copy(j).start()

    send_rest()

    @pl.loop(0, chunks)
    def _(c):
        turn(c)
        pl.when(c > 0)(functools.partial(dress, c, 0))
        for b in range(1, edge):
            dress(c, b)

    partial[...] = jnp.zeros_like(partial)
    for j in range(len(plane)):
        plane_copy(j).wait_send()
        plane_copy(j).wait_recv()

    def arrived(c, b):
        columns = pl.ds(0, full[b])
        others = received.at[c, b, :, pl.ds(0, depth - CHUNK), columns]
        pltpu.make_async_copy(others, others, recv_sem.at[c, b]).wait()
        mine = received.at[c, b, :, pl.ds(0, CHUNK), columns]
        pltpu.make_async_copy(mine, mine, own_sem.at[c, b]).wait()

    def add(i, first, lhs, rhs):
        rows = pl.ds(first, lhs.shape[1])
        for lo in range(0, slab.shape[-1], COLUMNS):
            partial[i, rows, lo:lo + COLUMNS] += lax.dot_general(
                lhs, rhs[:, lo:lo + COLUMNS], (((0,), (0,)), ((), ())),
                preferred_element_type=jnp.float32,
            )

    def contract_block(c, b):
        arrived(c, b)
        rhs = slab[c].reshape(depth, slab.shape[-1])

        @pl.loop(0, per)
        def _(i):
            add(i, b * BLOCK, received[c, b, i, :, 0:full[b]], rhs)

    contract_block(0, 0)

    @pl.loop(0, chunks)
    def _(c):
        contract_block(c, edge)

    others = unpacked.at[pl.ds(0, ng * nv - 1), pl.ds(0, kept)]
    pltpu.make_async_copy(others, others, rest_recv).wait()
    own_rest.wait()
    pl.loop(0, ng * nv)(unpack)

    @pl.loop(0, chunks)
    def _(c):
        rhs = slab[c].reshape(depth, slab.shape[-1])

        @pl.loop(0, per)
        def _(i):
            lhs = unpacked[:, c * per + i].reshape(depth, LANES)[:, 0:rest]
            add(i, nvirt - rest, lhs, rhs)

    @pl.loop(0, chunks)
    def _(c):
        pl.when(c > 0)(functools.partial(contract_block, c, 0))
        for b in range(1, edge - 1):
            contract_block(c, b)
        pl.when(c + 1 < chunks)(functools.partial(contract_block, c, edge - 1))

    arrived(chunks - 1, edge - 1)
    for b in range(blocks):
        sent = received.at[:, b, :, pl.ds(0, depth - CHUNK), pl.ds(0, full[b])]
        pltpu.make_async_copy(sent, sent, send_sem.at[b]).wait()
    pltpu.make_async_copy(others, others, rest_send).wait()


def finish_kernel(partial, received, slab, out, tail, sems):
    last, block = received.shape[0] - 1, received.shape[1] - 2
    per, nvirt = partial.shape[0], partial.shape[1]
    lo, hi = block * BLOCK, block * BLOCK + BLOCK
    copies = []

    def copy(src, dst):
        copies.append(pltpu.make_async_copy(src, dst, sems.at[len(copies)]))
        copies[-1].start()

    for i in range(per):
        copy(partial.at[i, 0:lo], out.at[i, 0:lo])
        copy(partial.at[i, hi:nvirt], out.at[i, hi:nvirt])
    rhs = slab[last].reshape(received.shape[3], slab.shape[-1])
    for i in range(per):
        tail[i] = partial[i, lo:hi, :] + lax.dot_general(
            received[last, block, i], rhs, (((0,), (0,)), ((), ())),
            preferred_element_type=jnp.float32,
        )
        copy(tail.at[i], out.at[i, lo:hi])
    for one in copies:
        one.wait()


def contract(ng, nv, vv_vectors, oo_vectors, ov_slab, amplitudes):
    local_count, nvirt = vv_vectors.shape[0], vv_vectors.shape[1]
    width = ov_slab.shape[1]
    devices = ng * nv
    inner = 2
    outer = nv // inner
    chunks = local_count // CHUNK
    blocks = -(-nvirt // BLOCK)
    per = I_ROWS // devices
    nocc = ng * amplitudes.shape[0]
    hbm = pl.BlockSpec(memory_space=pltpu.HBM)
    vmem = pl.BlockSpec(memory_space=pltpu.VMEM)
    dma = pltpu.SemaphoreType.DMA
    stay = functools.partial(pltpu.with_memory_space_constraint, memory_space=pltpu.HBM)
    partial, received, slab = pl.pallas_call(
        functools.partial(exchange_kernel, ng, nv, inner),
        out_shape=(
            jax.ShapeDtypeStruct((per, nvirt, width), jnp.float32),
            jax.ShapeDtypeStruct((chunks, blocks, per, devices * CHUNK, BLOCK), jnp.bfloat16),
            jax.ShapeDtypeStruct((chunks, ng, outer, inner * CHUNK, width), jnp.bfloat16),
        ),
        in_specs=[hbm, hbm, hbm, hbm],
        out_specs=(vmem, vmem, vmem),
        scratch_shapes=[
            pltpu.VMEM((devices, chunks * per, CHUNK, LANES), jnp.bfloat16),
            pltpu.VMEM((devices, chunks * per, CHUNK, LANES), jnp.bfloat16),
            pltpu.VMEM((blocks, CHUNK, BLOCK, nvirt), jnp.bfloat16),
            pltpu.VMEM((nocc, local_count, nocc), jnp.bfloat16),
            pltpu.VMEM((nocc * CHUNK, LANES), jnp.float32),
            pltpu.VMEM((CHUNK, I_ROWS, LANES), jnp.bfloat16),
            pltpu.VMEM((BLOCK // LANES, CHUNK * I_ROWS, LANES), jnp.float32),
            pltpu.VMEM((chunks, blocks, I_ROWS, CHUNK, BLOCK), jnp.bfloat16),
            pltpu.VMEM((ng,) + amplitudes.shape, jnp.bfloat16),
            pltpu.VMEM((nocc, nvirt), jnp.float32),
            pltpu.VMEM((nocc, nvirt), jnp.bfloat16),
            dma((blocks,)),
            dma((blocks,)),
            dma((chunks, blocks)),
            dma((chunks, blocks)),
            dma,
            dma((2,)),
            dma((2, 2, outer // 2)),
            dma((ng * inner - 1,)),
            dma((ng * inner - 1,)),
            dma,
            dma((ng, blocks)),
            dma((ng, blocks)),
            dma,
            dma,
            dma,
            dma,
        ],
        compiler_params=pltpu.CompilerParams(
            collective_id=0, has_side_effects=True, vmem_limit_bytes=LIMIT_MIB * 1024 * 1024
        ),
    )(
        stay(amplitudes), stay(jnp.transpose(oo_vectors, (1, 0, 2))),
        stay(ov_slab.reshape(chunks, CHUNK, width)), stay(vv_vectors),
    )
    return pl.pallas_call(
        finish_kernel,
        out_shape=jax.ShapeDtypeStruct((per, nvirt, width), jnp.float32),
        in_specs=[vmem, vmem, vmem],
        out_specs=hbm,
        scratch_shapes=[
            pltpu.VMEM((per, BLOCK, width), jnp.float32),
            dma((3 * per,)),
        ],
        compiler_params=pltpu.CompilerParams(vmem_limit_bytes=FINISH_MIB * 1024 * 1024),
    )(partial, received, slab).reshape(per * nvirt, width)


def plain(vv_vectors, oo_vectors, ov_slab, amps_all):
    local_count, nvirt = vv_vectors.shape[0], vv_vectors.shape[1]
    window = amps_all[:I_ROWS]
    direct_term = jnp.einsum("ib,pab->pia", window, vv_vectors, preferred_element_type=jnp.float32)
    hole_term = jnp.einsum(
        "pji,ja->pia", oo_vectors[:, :, :I_ROWS], amps_all, preferred_element_type=jnp.float32
    )
    dressed = (direct_term - hole_term).astype(jnp.bfloat16).reshape(local_count, I_ROWS * nvirt)
    regrouped = lax.all_to_all(dressed, ("grp", "vec"), split_axis=1, concat_axis=0, tiled=True)
    return lax.dot_general(
        regrouped,
        lax.all_gather(ov_slab, ("grp", "vec"), axis=0, tiled=True),
        (((0,), (0,)), ((), ())),
        preferred_element_type=jnp.float32,
    )


def solution(mesh):
    ng, nv = mesh.shape["grp"], mesh.shape["vec"]

    def shards(vv_vectors, oo_vectors, ov_slab, amplitudes):
        local_count, nvirt = vv_vectors.shape[0], vv_vectors.shape[1]
        fits = (
            I_ROWS % (ng * nv) == 0 and nv % 4 == 0 and local_count % CHUNK == 0 and nvirt % CHUNK == 0
            and LANES < nvirt % BLOCK < BLOCK
            and nvirt > 3 * BLOCK and local_count > 2 * CHUNK
            and oo_vectors.shape[1] <= LANES and ov_slab.shape[1] % COLUMNS == 0
        )
        if not fits:
            amps_all = lax.all_gather(amplitudes, "grp", axis=0, tiled=True)
            return plain(vv_vectors, oo_vectors, ov_slab, amps_all)
        return contract(ng, nv, vv_vectors, oo_vectors, ov_slab, amplitudes)

    return jax.shard_map(
        shards,
        mesh=mesh,
        in_specs=(
            P(("grp", "vec"), None, None),
            P(("grp", "vec"), None, None),
            P(("grp", "vec"), None),
            P("grp", None),
        ),
        out_specs=P(("grp", "vec"), None),
        check_vma=False,
    )
```
